32 devices in a mesh: expert: 8 (over y, x, core), dp: 4 (over z).
Axes of the slice: x: 2, y: 2, z: 4, core: 2. Of those that a mesh axis runs over, the one named last changes fastest.
Arguments:
- trunk: bfloat16 [768, 4096], P(('dp', 'expert')), may hold values from -6 to 6
- w_first: bfloat16 [8, 4096, 2048], P('expert'), may hold values from -0.09375 to 0.09375
- w_second: bfloat16 [8, 2048, 1024], P('expert'), may hold values from -0.125 to 0.125
- gates: bfloat16 [8, 8, 768], P('expert', None, 'dp'), may hold values from 0.049804688 to 1
- d_mixed: bfloat16 [768, 8, 1024], P(('dp', 'expert')), may hold values from -6 to 6
Outputs:
- mixed: bfloat16 [768, 8, 1024], P(('dp', 'expert'))
- d_trunk: bfloat16 [768, 4096], P(('dp', 'expert'))
- d_gates: bfloat16 [8, 8, 768], P('expert', None, 'dp')
- d_w_first: bfloat16 [8, 4096, 2048], P('expert', 'dp')
- d_w_second: bfloat16 [8, 2048, 1024], P('expert', 'dp')
The draws below stay inside these ranges and needn't reach their ends.
All inputs are finite; a program needn't handle non-finite values.
Results may differ from the reference program's by a relative error of at most 0.015.
Values may be sent and summed in bfloat16 or wider, within the bound.
A program may use at most 128 MiB of HBM per device.

```python
import math
import jax
import jax.numpy as jnp
from jax import lax

D = 4096
H = 2048
O = 1024
TASKS = 8
EXPERTS = 8
GROUP = 192
SAMPLES = 768
N_DP = 4


def level_of(stream_key, shape, shards, smallest, high):
    factor_of, own = 1.0, jax.random.fold_in(stream_key, 6)
    for dim, blocks in shards:
        steps = jnp.exp(jax.random.uniform(jax.random.fold_in(own, dim), (blocks,), jnp.float32, smallest / len(shards), high / len(shards)))
        factor_of = factor_of * jnp.repeat(steps, shape[dim] // blocks).reshape([-1 if axis == dim else 1 for axis in range(len(shape))])
    return factor_of


def normal_values(own_key, dims, width, bound, cuts=(), dtype=jnp.bfloat16):
    entries = width * jax.random.normal(own_key, dims, jnp.float32)
    if cuts:
        entries = entries * level_of(own_key, dims, cuts, -0.22, 0.18)
    return jnp.clip(entries, -bound, bound).astype(dtype)


def setup_inputs(seed: int = 0) -> dict:
    arg_keys = jax.random.split(jax.random.key(seed), 6)
    return {
        "trunk": normal_values(arg_keys[0], (SAMPLES, D), 1.0, 6.0, ((0, 32),)),
        "w_first": normal_values(arg_keys[1], (EXPERTS, D, H), D ** -0.5, 0.09375, ((0, 8),)),
        "w_second": normal_values(arg_keys[2], (EXPERTS, H, O), H ** -0.5, 0.125, ((0, 8),)),
        "gates": jnp.clip(jnp.exp(math.log(1.0) - 2.9996462 * jax.random.uniform(arg_keys[3], (EXPERTS, TASKS, SAMPLES), jnp.float32) ** level_of(arg_keys[3], (EXPERTS, TASKS, SAMPLES), ((0, 8), (2, 4)), -0.2, 0.2)), 0.049804688, 1.0).astype(jnp.bfloat16),
        "d_mixed": normal_values(arg_keys[4], (SAMPLES, TASKS, O), 1.0, 6.0, ((0, 32),)),
    }


def reference(trunk, w_first, w_second, gates, d_mixed):
    cot = d_mixed.astype(jnp.float32)
    trunk_blocks = trunk.astype(jnp.float32).reshape(N_DP, GROUP, D)

    def per_expert(carry, packed):
        mixed_acc, trunk_acc = carry
        first, second, gate = packed
        pre = jnp.dot(trunk, first, preferred_element_type=jnp.float32)
        hidden = jax.nn.silu(pre).astype(jnp.bfloat16)
        output = jnp.dot(hidden, second, preferred_element_type=jnp.float32).astype(jnp.bfloat16)
        weight = gate.astype(jnp.float32)
        out_f = output.astype(jnp.float32)
        mixed_acc = mixed_acc + weight.T[:, :, None] * out_f[:, None, :]
        d_output = jnp.einsum("ts,sto->so", weight, cot).astype(jnp.bfloat16)
        d_gate = jnp.einsum("sto,so->ts", cot, out_f).astype(jnp.bfloat16)
        d_hidden = lax.dot_general(d_output, second, (((1,), (1,)), ((), ())), preferred_element_type=jnp.float32)
        sig = jax.nn.sigmoid(pre)
        d_pre = (d_hidden * sig * (1.0 + pre * (1.0 - sig))).astype(jnp.bfloat16)
        trunk_acc = trunk_acc + lax.dot_general(d_pre, first, (((1,), (1,)), ((), ())), preferred_element_type=jnp.float32)
        pre_blocks = d_pre.astype(jnp.float32).reshape(N_DP, GROUP, H)
        part_first = jnp.einsum("gsd,gsh->gdh", trunk_blocks, pre_blocks).astype(jnp.bfloat16)
        part_first = lax.optimization_barrier(part_first).astype(jnp.float32)
        d_first = jnp.sum(part_first, axis=0).astype(jnp.bfloat16)
        hid_blocks = hidden.astype(jnp.float32).reshape(N_DP, GROUP, H)
        dout_blocks = d_output.astype(jnp.float32).reshape(N_DP, GROUP, O)
        part_second = jnp.einsum("gsh,gso->gho", hid_blocks, dout_blocks).astype(jnp.bfloat16)
        part_second = lax.optimization_barrier(part_second).astype(jnp.float32)
        d_second = jnp.sum(part_second, axis=0).astype(jnp.bfloat16)
        return (mixed_acc, trunk_acc), (d_gate, d_first, d_second)

    init = (jnp.zeros((SAMPLES, TASKS, O), jnp.float32), jnp.zeros((SAMPLES, D), jnp.float32))
    (mixed_acc, trunk_acc), (d_gates, d_w_first, d_w_second) = lax.scan(per_expert, init, (w_first, w_second, gates))
    return (mixed_acc.astype(jnp.bfloat16), trunk_acc.astype(jnp.bfloat16), d_gates, d_w_first, d_w_second)
```

```python
import jax
import jax.numpy as jnp
from jax import lax
from jax.sharding import PartitionSpec as P

F32 = jnp.float32
BF16 = jnp.bfloat16


def on_device(trunk, w_first, w_second, gates, d_mixed):
    rank = lax.axis_index("dp")
    first = w_first[0]
    second = w_second[0]
    gate_here = gates[0]
    n_dp = lax.axis_size("dp")
    depth = first.shape[0] // n_dp
    units = second.shape[0] // n_dp
    group = gate_here.shape[1]

    rows_all = lax.all_gather(trunk, ("dp", "expert"), axis=0, tiled=True)
    gates_each = lax.all_to_all(gate_here.T[None], "expert", split_axis=1, concat_axis=0, tiled=True)
    d_out_each = jnp.einsum(
        "ert,rto->ero", gates_each, d_mixed, preferred_element_type=F32
    ).astype(BF16)
    d_output = lax.all_to_all(d_out_each, "expert", split_axis=0, concat_axis=1, tiled=True)[0]
    d_output_all = lax.all_gather(d_output, "dp", axis=0, tiled=True)

    pre = jnp.dot(rows_all, first, preferred_element_type=F32)
    pre_here = lax.dynamic_slice_in_dim(pre, rank * group, group, 0)
    hidden_here = jax.nn.silu(pre_here).astype(BF16)
    output = jnp.dot(hidden_here, second, preferred_element_type=F32).astype(BF16)
    outs_each = lax.all_to_all(output[None], "expert", split_axis=1, concat_axis=0, tiled=True)

    d_hidden = lax.dot_general(
        d_output_all, second, (((1,), (1,)), ((), ())), preferred_element_type=F32
    )
    sig = jax.nn.sigmoid(pre)
    d_pre = (d_hidden * sig * (1.0 + pre * (1.0 - sig))).astype(BF16)
    d_pre_here = lax.dynamic_slice_in_dim(d_pre, rank * group, group, 0)
    d_trunk = lax.psum_scatter(
        lax.dot_general(
            d_pre_here, first, (((1,), (1,)), ((), ())), preferred_element_type=F32
        ).astype(BF16),
        "expert",
        scatter_dimension=0,
        tiled=True,
    )

    mixed = jnp.einsum(
        "ert,ero->rto", gates_each, outs_each, preferred_element_type=F32
    ).astype(BF16)
    d_gate_each = jnp.einsum(
        "rto,ero->ert", d_mixed, outs_each, preferred_element_type=F32
    ).astype(BF16)
    back_gate = lax.all_to_all(d_gate_each, "expert", split_axis=0, concat_axis=1, tiled=True)
    d_gate = back_gate[0].T[None]

    columns = lax.dynamic_slice_in_dim(rows_all, rank * depth, depth, 1)
    d_first = lax.dot_general(
        columns, d_pre, (((0,), (0,)), ((), ())), preferred_element_type=F32
    ).astype(BF16)
    some_pre = lax.dynamic_slice_in_dim(pre, rank * units, units, 1)
    some_hidden = jax.nn.silu(some_pre).astype(BF16)
    d_second = lax.dot_general(
        some_hidden, d_output_all, (((0,), (0,)), ((), ())), preferred_element_type=F32
    ).astype(BF16)
    return (mixed, d_trunk, d_gate, d_first[None], d_second[None])


def solution(mesh):
    in_specs = (
        P(("dp", "expert"), None),
        P("expert", None, None),
        P("expert", None, None),
        P("expert", None, "dp"),
        P(("dp", "expert"), None, None),
    )
    out_specs = (
        P(("dp", "expert"), None, None),
        P(("dp", "expert"), None),
        P("expert", None, "dp"),
        P("expert", "dp", None),
        P("expert", "dp", None),
    )
    return jax.shard_map(
        on_device, mesh=mesh, in_specs=in_specs, out_specs=out_specs, check_vma=False
    )
```

```python
import functools

import jax
import jax.numpy as jnp
from jax import lax
from jax.experimental import pallas as pl
from jax.experimental.pallas import tpu as pltpu
from jax.sharding import PartitionSpec as P

F32 = jnp.float32
BF16 = jnp.bfloat16


MESH = pl.DeviceIdType.MESH


def gather_kernel(n_e, n_d, trunk, gates, cot, first, second, rows, d_out, pre, gate_each,
                  outs, weights, later, hidden, made, m_send, m_recv, later_sem, piece, block, tall, w_sem, load_sem, store_sem,
                  g_send, g_recv, t_send, t_recv, o_send, o_recv, z_send, z_recv,
                  own_sem):
    e = lax.axis_index("expert")
    z = lax.axis_index("dp")
    partner = e + 1 - 2 * lax.rem(e, 2)
    pairs = n_e // 2

    def plane(s):
        return lax.rem(e + s, n_e)

    def along(i):
        return lax.rem(z + i, n_d)

    def remote(src, dst, send, recv, where):
        return pltpu.make_async_remote_copy(
            src_ref=src, dst_ref=dst, send_sem=send, recv_sem=recv,
            device_id=where, device_id_type=MESH)

    load_weights = pltpu.make_async_copy(first, weights, w_sem)
    load_weights.start()
    load_later = pltpu.make_async_copy(second, later, later_sem)
    load_later.start()

    barrier = pltpu.get_barrier_semaphore()
    for s in range(1, n_e):
        pl.semaphore_signal(barrier, inc=1, device_id={"expert": plane(s)}, device_id_type=MESH)
    for i in range(1, n_d):
        pl.semaphore_signal(barrier, inc=1, device_id={"dp": along(i)}, device_id_type=MESH)
    pl.semaphore_wait(barrier, n_e - 1 + n_d - 1)

    sent = []

    def go(copy):
        copy.start()
        sent.append(copy)

    for s in range(1, n_e):
        j = plane(s)
        go(remote(gates.at[j], gate_each.at[e], g_send.at[s], g_recv.at[e], {"expert": j}))
    own_gate = pltpu.make_async_copy(gates.at[e], gate_each.at[e], own_sem.at[0])
    own_gate.start()
    own_rows = pltpu.make_async_copy(trunk, rows.at[z, e], own_sem.at[1])
    own_rows.start()

    def spread(i):
        zi = along(i)
        src = trunk if i == 0 else rows.at[zi, e]
        for s in range(1, pairs):
            go(remote(src, rows.at[zi, e], t_send.at[i, s], t_recv.at[zi, e],
                      {"expert": plane(2 * s)}))
        go(remote(src, rows.at[zi, e], t_send.at[i, 0], t_recv.at[zi, e], {"expert": partner}))

    def arrived(zi, j):
        remote(trunk, rows.at[zi, j], t_send.at[0, 0], t_recv.at[zi, j],
               {"expert": partner}).wait_recv()

    for i in range(1, n_d):
        go(remote(trunk, rows.at[z, e], t_send.at[i, n_e - 1], t_recv.at[z, e], {"dp": along(i)}))
    spread(0)

    for s in range(1, n_e):
        j = plane(s)
        remote(gates.at[j], gate_each.at[j], g_send.at[0], g_recv.at[j], {"expert": j}).wait_recv()
    own_gate.wait()
    tasks = cot.shape[0]

    @pl.loop(0, n_e)
    def _(j):
        weight = gate_each[j]
        total = weight[:, 0:1] * cot[0].astype(F32)
        for t in range(1, tasks):
            total = total + weight[:, t:t + 1] * cot[t].astype(F32)
        piece[j] = total.astype(BF16)

    own_piece = pltpu.make_async_copy(piece.at[e], d_out.at[z, e], own_sem.at[2])
    own_piece.start()
    for s in range(1, n_e):
        j = plane(s)
        go(remote(piece.at[j], d_out.at[z, e], o_send.at[s], o_recv.at[e], {"expert": j}))

    def send_outputs():
        own_made.start()
        for s in range(1, n_e):
            j = plane(s)
            go(remote(made.at[j], outs.at[e], m_send.at[s], m_recv.at[e], {"expert": j}))

    own_made = pltpu.make_async_copy(made.at[e], outs.at[e], own_sem.at[3])
    stores = []
    for i in range(n_d):
        zi = along(i)
        if i + 1 < n_d:
            arrived(along(i + 1), e)
            spread(i + 1)
        if i == 1:
            send_outputs()
        if i == 0:
            for s in range(1, n_e):
                j = plane(s)
                remote(piece.at[j], d_out.at[z, j], o_send.at[0], o_recv.at[j],
                       {"expert": j}).wait_recv()
            own_piece.wait()
            for k in range(1, n_d):
                go(remote(d_out.at[z], d_out.at[z], z_send.at[k], z_recv.at[z], {"dp": along(k)}))
            own_rows.wait()
        for s in range(1, pairs):
            j = plane(2 * s)
            arrived(zi, j)
            go(remote(rows.at[zi, j], rows.at[zi, j], t_send.at[i, pairs - 1 + s],
                      t_recv.at[zi, j], {"expert": partner}))
        for s in range(pairs):
            arrived(zi, lax.rem(partner + 2 * s, n_e))
        load = pltpu.make_async_copy(rows.at[zi], block, load_sem)
        load.start()
        if i == 0:
            load_weights.wait()
        else:
            stores[-1].wait()
        load.wait()
        height = block.shape[0] * block.shape[1]
        tile = 256
        left = block[...].reshape(height, block.shape[2])

        @pl.loop(0, tall.shape[1] // tile)
        def _(c):
            here = pl.ds(pl.multiple_of(c * tile, tile), tile)
            value = jnp.dot(left, weights[:, here], preferred_element_type=F32)
            tall[:, here] = value
            if i == 0:
                hidden[:, here] = (value * jax.nn.sigmoid(value)).astype(BF16)

        store = pltpu.make_async_copy(tall, pre.at[zi], store_sem)
        store.start()
        stores.append(store)
        if i == 0:
            load_later.wait()

            @pl.loop(0, made.shape[2] // tile)
            def _(c):
                here = pl.ds(pl.multiple_of(c * tile, tile), tile)
                value = jnp.dot(hidden[...], later[:, here], preferred_element_type=F32)
                made[:, :, here] = value.astype(BF16).reshape(n_e, -1, tile)

    stores[-1].wait()
    if n_d == 1:
        send_outputs()
    own_made.wait()
    for s in range(1, n_e):
        j = plane(s)
        remote(made.at[j], outs.at[j], m_send.at[0], m_recv.at[j], {"expert": j}).wait_recv()
    for i in range(1, n_d):
        zi = along(i)
        remote(d_out.at[zi], d_out.at[zi], z_send.at[0], z_recv.at[zi], {"dp": zi}).wait_recv()
    for copy in sent:
        copy.wait_send()


def gather_all(trunk, gates, cot, first, second):
    n_e, n_d = lax.axis_size("expert"), lax.axis_size("dp")
    share, depth = trunk.shape
    width = first.shape[1]
    out = cot.shape[2]
    anywhere = pl.BlockSpec(memory_space=pl.ANY)
    hbm = pl.BlockSpec(memory_space=pltpu.HBM)
    vmem = pl.BlockSpec(memory_space=pltpu.VMEM)
    dma = pltpu.SemaphoreType.DMA
    return pl.pallas_call(
        functools.partial(gather_kernel, n_e, n_d),
        out_shape=(
            jax.ShapeDtypeStruct((n_d, n_e, share, depth), BF16),
            jax.ShapeDtypeStruct((n_d, n_e, share, out), BF16),
            jax.ShapeDtypeStruct((n_d, n_e * share, width), F32),
            jax.ShapeDtypeStruct(gates.shape, F32),
            jax.ShapeDtypeStruct((n_e, share, out), BF16),
        ),
        in_specs=[vmem, vmem, vmem, hbm, hbm],
        out_specs=(hbm, hbm, hbm, vmem, hbm),
        scratch_shapes=[
            pltpu.VMEM(first.shape, BF16),
            pltpu.VMEM(second.shape, BF16),
            pltpu.VMEM((n_e * share, width), BF16),
            pltpu.VMEM((n_e, share, out), BF16),
            dma((n_e,)), dma((n_e,)), dma,
            pltpu.VMEM((n_e, share, out), BF16),
            pltpu.VMEM((n_e, share, depth), BF16),
            pltpu.VMEM((n_e * share, width), F32),
            dma, dma, dma,
            dma((n_e,)), dma((n_e,)),
            dma((n_d, n_e)), dma((n_d, n_e)),
            dma((n_e,)), dma((n_e,)),
            dma((n_d,)), dma((n_d,)),
            dma((4,)),
        ],
        compiler_params=pltpu.CompilerParams(
            collective_id=0, has_side_effects=True, vmem_limit_bytes=48 * 1024 * 1024),
    )(trunk, gates, cot, first, second)


def return_kernel(n_e, d_pre, first, d_gate, d_trunk, gate_back, weights, part, got,
                  w_sem, p_send, p_recv, g_send, g_recv, own_sem):
    e = lax.axis_index("expert")
    tiles, tile, _ = weights.shape

    def plane(s):
        return lax.rem(e + s, n_e)

    def remote(src, dst, send, recv, j):
        return pltpu.make_async_remote_copy(
            src_ref=src, dst_ref=dst, send_sem=send, recv_sem=recv,
            device_id={"expert": j}, device_id_type=MESH)

    def load(c):
        return pltpu.make_async_copy(first.at[c], weights.at[c], w_sem.at[c])

    for c in range(tiles):
        load(c).start()
    barrier = pltpu.get_barrier_semaphore()
    for s in range(1, n_e):
        pl.semaphore_signal(barrier, inc=1, device_id={"expert": plane(s)}, device_id_type=MESH)
    pl.semaphore_wait(barrier, n_e - 1)

    own = pltpu.make_async_copy(d_gate.at[e], gate_back.at[e], own_sem)
    own.start()

    def gate_out(s):
        j = plane(s)
        return remote(d_gate.at[j], gate_back.at[e], g_send.at[s], g_recv.at[e], j)

    def part_out(c, s):
        j = plane(s)
        return remote(part.at[c, j], got.at[c, e], p_send.at[c, s], p_recv.at[c, e], j)

    for s in range(1, n_e):
        gate_out(s).start()

    def compute(c):
        load(c).wait()
        value = lax.dot_general(
            d_pre[...], weights[c], (((1,), (1,)), ((), ())), preferred_element_type=F32)
        part[c] = value.astype(BF16).reshape(n_e, -1, tile)

    def send(c):
        for s in range(1, n_e):
            part_out(c, s).start()

    compute(0)

    @pl.loop(1, tiles)
    def _(c):
        send(c - 1)
        compute(c)

    send(tiles - 1)

    @pl.loop(0, tiles)
    def _(c):
        total = part[c, e].astype(F32)
        for s in range(1, n_e):
            j = plane(s)
            remote(part.at[c, j], got.at[c, j], p_send.at[c, 0], p_recv.at[c, j], j).wait_recv()
            total = total + got[c, j].astype(F32)
        d_trunk[:, pl.ds(pl.multiple_of(c * tile, tile), tile)] = total.astype(BF16)

    own.wait()
    for s in range(1, n_e):
        j = plane(s)
        remote(d_gate.at[j], gate_back.at[j], g_send.at[0], g_recv.at[j], j).wait_recv()
    for s in range(1, n_e):
        gate_out(s).wait_send()

    @pl.loop(0, tiles)
    def _(c):
        for s in range(1, n_e):
            part_out(c, s).wait_send()


def return_all(d_pre, first, d_gate):
    n_e = lax.axis_size("expert")
    tile = 512
    depth, width = first.shape
    tiles = depth // tile
    share = d_pre.shape[0] // n_e
    hbm = pl.BlockSpec(memory_space=pltpu.HBM)
    vmem = pl.BlockSpec(memory_space=pltpu.VMEM)
    dma = pltpu.SemaphoreType.DMA
    return pl.pallas_call(
        functools.partial(return_kernel, n_e),
        out_shape=(
            jax.ShapeDtypeStruct((share, depth), BF16),
            jax.ShapeDtypeStruct(d_gate.shape, F32),
        ),
        in_specs=[vmem, hbm, vmem],
        out_specs=(vmem, vmem),
        scratch_shapes=[
            pltpu.VMEM((tiles, tile, width), BF16),
            pltpu.VMEM((tiles, n_e, share, tile), BF16),
            pltpu.VMEM((tiles, n_e, share, tile), BF16),
            dma((tiles,)),
            dma((tiles, n_e)), dma((tiles, n_e)),
            dma((n_e,)), dma((n_e,)), dma,
        ],
        compiler_params=pltpu.CompilerParams(
            collective_id=1, has_side_effects=True, vmem_limit_bytes=48 * 1024 * 1024),
    )(d_pre, first.reshape(tiles, tile, width), d_gate)


def on_device(trunk, w_first, w_second, gates, d_mixed):
    rank = lax.axis_index("dp")
    first = w_first[0]
    second = w_second[0]
    gate_here = gates[0]
    n_dp = lax.axis_size("dp")
    depth = first.shape[0] // n_dp
    units = second.shape[0] // n_dp
    group = gate_here.shape[1]

    n_e = lax.axis_size("expert")
    gate_parts = gate_here.T.astype(F32).reshape(n_e, -1, gate_here.shape[0])
    rows_all, d_output_all, pre, gates_each, outs_each = gather_all(
        trunk, gate_parts, jnp.transpose(d_mixed, (1, 0, 2)), first, second)
    rows_all = rows_all.reshape(-1, trunk.shape[1])
    d_output_all = d_output_all.reshape(-1, second.shape[1])
    pre = pre.reshape(-1, first.shape[1])
    gates_each = gates_each.astype(BF16)
    d_hidden = lax.dot_general(
        d_output_all, second, (((1,), (1,)), ((), ())), preferred_element_type=F32
    )
    sig = jax.nn.sigmoid(pre)
    d_pre = (d_hidden * sig * (1.0 + pre * (1.0 - sig))).astype(BF16)
    d_pre_here = lax.dynamic_slice_in_dim(d_pre, rank * group, group, 0)
    mixed = jnp.einsum(
        "ert,ero->rto", gates_each, outs_each, preferred_element_type=F32
    ).astype(BF16)
    d_gate_each = jnp.einsum(
        "rto,ero->ert", d_mixed, outs_each, preferred_element_type=F32
    ).astype(BF16)
    d_trunk, back_gate = return_all(d_pre_here, first, d_gate_each.astype(F32))
    d_gate = back_gate.reshape(group, -1).T.astype(BF16)[None]

    columns = lax.dynamic_slice_in_dim(rows_all, rank * depth, depth, 1)
    d_first = lax.dot_general(
        columns, d_pre, (((0,), (0,)), ((), ())), preferred_element_type=F32
    ).astype(BF16)
    some_pre = lax.dynamic_slice_in_dim(pre, rank * units, units, 1)
    some_hidden = jax.nn.silu(some_pre).astype(BF16)
    d_second = lax.dot_general(
        some_hidden, d_output_all, (((0,), (0,)), ((), ())), preferred_element_type=F32
    ).astype(BF16)
    return (mixed, d_trunk, d_gate, d_first[None], d_second[None])


def solution(mesh):
    in_specs = (
        P(("dp", "expert"), None),
        P("expert", None, None),
        P("expert", None, None),
        P("expert", None, "dp"),
        P(("dp", "expert"), None, None),
    )
    out_specs = (
        P(("dp", "expert"), None, None),
        P(("dp", "expert"), None),
        P("expert", None, "dp"),
        P("expert", "dp", None),
        P("expert", "dp", None),
    )
    return jax.shard_map(
        on_device, mesh=mesh, in_specs=in_specs, out_specs=out_specs, check_vma=False
    )
```

```python
import functools

import jax
import jax.numpy as jnp
from jax import lax
from jax.experimental import pallas as pl
from jax.experimental.pallas import tpu as pltpu
from jax.sharding import PartitionSpec as P

F32 = jnp.float32
BF16 = jnp.bfloat16


MESH = pl.DeviceIdType.MESH


def gather_kernel(n_e, n_d, trunk, gates, cot, first, second, rows, d_out, pre, gate_each,
                  outs, weights, later, hidden, made, m_send, m_recv, later_sem, piece, block, tall, w_sem, load_sem, store_sem,
                  g_send, g_recv, t_send, t_recv, o_send, o_recv, z_send, z_recv,
                  own_sem):
    e = lax.axis_index("expert")
    z = lax.axis_index("dp")
    partner = e + 1 - 2 * lax.rem(e, 2)
    pairs = n_e // 2

    def plane(s):
        return lax.rem(e + s, n_e)

    def along(i):
        return lax.rem(z + i, n_d)

    def remote(src, dst, send, recv, where):
        return pltpu.make_async_remote_copy(
            src_ref=src, dst_ref=dst, send_sem=send, recv_sem=recv,
            device_id=where, device_id_type=MESH)

    load_weights = pltpu.make_async_copy(first, weights, w_sem)
    load_weights.start()
    load_later = pltpu.make_async_copy(second, later, later_sem)
    load_later.start()

    barrier = pltpu.get_barrier_semaphore()
    for s in range(1, n_e):
        pl.semaphore_signal(barrier, inc=1, device_id={"expert": plane(s)}, device_id_type=MESH)
    for i in range(1, n_d):
        pl.semaphore_signal(barrier, inc=1, device_id={"dp": along(i)}, device_id_type=MESH)
    pl.semaphore_wait(barrier, n_e - 1 + n_d - 1)

    sent = []

    def go(copy):
        copy.start()
        sent.append(copy)

    for s in range(1, n_e):
        j = plane(s)
        go(remote(gates.at[j], gate_each.at[e], g_send.at[s], g_recv.at[e], {"expert": j}))
    own_gate = pltpu.make_async_copy(gates.at[e], gate_each.at[e], own_sem.at[0])
    own_gate.start()
    own_rows = pltpu.make_async_copy(trunk, rows.at[z, e], own_sem.at[1])
    own_rows.start()

    def spread(i):
        zi = along(i)
        src = trunk if i == 0 else rows.at[zi, e]
        for s in range(1, pairs):
            go(remote(src, rows.at[zi, e], t_send.at[i, s], t_recv.at[zi, e],
                      {"expert": plane(2 * s)}))
        go(remote(src, rows.at[zi, e], t_send.at[i, 0], t_recv.at[zi, e], {"expert": partner}))

    def arrived(zi, j):
        remote(trunk, rows.at[zi, j], t_send.at[0, 0], t_recv.at[zi, j],
               {"expert": partner}).wait_recv()

    for i in range(1, n_d):
        go(remote(trunk, rows.at[z, e], t_send.at[i, n_e - 1], t_recv.at[z, e], {"dp": along(i)}))
    spread(0)

    for s in range(1, n_e):
        j = plane(s)
        remote(gates.at[j], gate_each.at[j], g_send.at[0], g_recv.at[j], {"expert": j}).wait_recv()
    own_gate.wait()
    tasks = cot.shape[0]

    @pl.loop(0, n_e)
    def _(j):
        weight = gate_each[j]
        total = weight[:, 0:1] * cot[0].astype(F32)
        for t in range(1, tasks):
            total = total + weight[:, t:t + 1] * cot[t].astype(F32)
        piece[j] = total.astype(BF16)

    own_piece = pltpu.make_async_copy(piece.at[e], d_out.at[z, e], own_sem.at[2])
    own_piece.start()
    for s in range(1, n_e):
        j = plane(s)
        go(remote(piece.at[j], d_out.at[z, e], o_send.at[s], o_recv.at[e], {"expert": j}))

    def send_outputs():
        own_made.start()
        for s in range(1, n_e):
            j = plane(s)
            go(remote(made.at[j], outs.at[e], m_send.at[s], m_recv.at[e], {"expert": j}))

    own_made = pltpu.make_async_copy(made.at[e], outs.at[e], own_sem.at[3])
    stores = []
    for i in range(n_d):
        zi = along(i)
        if i + 1 < n_d:
            arrived(along(i + 1), e)
            spread(i + 1)
        if i == 1:
            send_outputs()
        if i == 0:
            for s in range(1, n_e):
                j = plane(s)
                remote(piece.at[j], d_out.at[z, j], o_send.at[0], o_recv.at[j],
                       {"expert": j}).wait_recv()
            own_piece.wait()
            for k in range(1, n_d):
                go(remote(d_out.at[z], d_out.at[z], z_send.at[k], z_recv.at[z], {"dp": along(k)}))
            own_rows.wait()
        for s in range(1, pairs):
            j = plane(2 * s)
            arrived(zi, j)
            go(remote(rows.at[zi, j], rows.at[zi, j], t_send.at[i, pairs - 1 + s],
                      t_recv.at[zi, j], {"expert": partner}))
        for s in range(pairs):
            arrived(zi, lax.rem(partner + 2 * s, n_e))
        load = pltpu.make_async_copy(rows.at[zi], block, load_sem)
        load.start()
        if i == 0:
            load_weights.wait()
        else:
            stores[-1].wait()
        load.wait()
        height = block.shape[0] * block.shape[1]
        tile = 256
        left = block[...].reshape(height, block.shape[2])

        @pl.loop(0, tall.shape[1] // tile)
        def _(c):
            here = pl.ds(pl.multiple_of(c * tile, tile), tile)
            value = jnp.dot(left, weights[:, here], preferred_element_type=F32)
            tall[:, here] = value
            if i == 0:
                hidden[:, here] = (value * jax.nn.sigmoid(value)).astype(BF16)

        store = pltpu.make_async_copy(tall, pre.at[zi], store_sem)
        store.start()
        stores.append(store)
        if i == 0:
            load_later.wait()

            @pl.loop(0, made.shape[2] // tile)
            def _(c):
                here = pl.ds(pl.multiple_of(c * tile, tile), tile)
                value = jnp.dot(hidden[...], later[:, here], preferred_element_type=F32)
                made[:, :, here] = value.astype(BF16).reshape(n_e, -1, tile)

    stores[-1].wait()
    if n_d == 1:
        send_outputs()
    own_made.wait()
    for s in range(1, n_e):
        j = plane(s)
        remote(made.at[j], outs.at[j], m_send.at[0], m_recv.at[j], {"expert": j}).wait_recv()
    for i in range(1, n_d):
        zi = along(i)
        remote(d_out.at[zi], d_out.at[zi], z_send.at[0], z_recv.at[zi], {"dp": zi}).wait_recv()
    for copy in sent:
        copy.wait_send()


def gather_all(trunk, gates, cot, first, second):
    n_e, n_d = lax.axis_size("expert"), lax.axis_size("dp")
    share, depth = trunk.shape
    width = first.shape[1]
    out = cot.shape[2]
    anywhere = pl.BlockSpec(memory_space=pl.ANY)
    hbm = pl.BlockSpec(memory_space=pltpu.HBM)
    vmem = pl.BlockSpec(memory_space=pltpu.VMEM)
    dma = pltpu.SemaphoreType.DMA
    return pl.pallas_call(
        functools.partial(gather_kernel, n_e, n_d),
        out_shape=(
            jax.ShapeDtypeStruct((n_d, n_e, share, depth), BF16),
            jax.ShapeDtypeStruct((n_d, n_e, share, out), BF16),
            jax.ShapeDtypeStruct((n_d, n_e * share, width), F32),
            jax.ShapeDtypeStruct(gates.shape, F32),
            jax.ShapeDtypeStruct((n_e, share, out), BF16),
        ),
        in_specs=[vmem, vmem, vmem, hbm, hbm],
        out_specs=(hbm, hbm, hbm, vmem, hbm),
        scratch_shapes=[
            pltpu.VMEM(first.shape, BF16),
            pltpu.VMEM(second.shape, BF16),
            pltpu.VMEM((n_e * share, width), BF16),
            pltpu.VMEM((n_e, share, out), BF16),
            dma((n_e,)), dma((n_e,)), dma,
            pltpu.VMEM((n_e, share, out), BF16),
            pltpu.VMEM((n_e, share, depth), BF16),
            pltpu.VMEM((n_e * share, width), F32),
            dma, dma, dma,
            dma((n_e,)), dma((n_e,)),
            dma((n_d, n_e)), dma((n_d, n_e)),
            dma((n_e,)), dma((n_e,)),
            dma((n_d,)), dma((n_d,)),
            dma((4,)),
        ],
        compiler_params=pltpu.CompilerParams(
            collective_id=0, has_side_effects=True, vmem_limit_bytes=48 * 1024 * 1024),
    )(trunk, gates, cot, first, second)


def return_kernel(n_e, d_pre, first, d_gate, d_trunk, gate_back, weights, part, near, pair, got,
                  w_sem, n_send, n_recv, p_send, p_recv, g_send, g_recv, own_sem):
    e = lax.axis_index("expert")
    core, seat, pairs = lax.rem(e, 2), e // 2, n_e // 2
    partner = e + 1 - 2 * core
    tiles, tile, _ = weights.shape

    def plane(s):
        return lax.rem(e + s, n_e)

    def remote(src, dst, send, recv, j):
        return pltpu.make_async_remote_copy(
            src_ref=src, dst_ref=dst, send_sem=send, recv_sem=recv,
            device_id={"expert": j}, device_id_type=MESH)

    def load(c):
        return pltpu.make_async_copy(first.at[c], weights.at[c], w_sem.at[c])

    for c in range(tiles):
        load(c).start()
    barrier = pltpu.get_barrier_semaphore()
    for s in range(1, n_e):
        pl.semaphore_signal(barrier, inc=1, device_id={"expert": plane(s)}, device_id_type=MESH)
    pl.semaphore_wait(barrier, n_e - 1)

    own = pltpu.make_async_copy(d_gate.at[e], gate_back.at[e], own_sem)
    own.start()

    def gate_out(s):
        j = plane(s)
        return remote(d_gate.at[j], gate_back.at[e], g_send.at[s], g_recv.at[e], j)

    def near_out(c):
        return remote(part.at[c, :, 1 - core], near.at[c], n_send.at[c], n_recv.at[c], partner)

    def part_out(c, s):
        k = lax.rem(seat + s, pairs)
        return remote(pair.at[c, k], got.at[c, seat], p_send.at[c, s], p_recv.at[c, seat],
                      2 * k + core)

    for s in range(1, n_e):
        gate_out(s).start()

    def compute(c):
        load(c).wait()
        value = lax.dot_general(
            d_pre[...], weights[c], (((1,), (1,)), ((), ())), preferred_element_type=F32)
        part[c] = value.astype(BF16).reshape(pairs, 2, -1, tile)

    def combine(c):
        near_out(c).wait_recv()
        pair[c] = (part[c, :, core].astype(F32) + near[c].astype(F32)).astype(BF16)

    def send(c):
        for s in range(1, pairs):
            part_out(c, s).start()

    compute(0)
    near_out(0).start()
    compute(1)
    combine(0)

    @pl.loop(2, tiles)
    def _(c):
        near_out(c - 1).start()
        send(c - 2)
        compute(c)
        combine(c - 1)

    near_out(tiles - 1).start()
    send(tiles - 2)
    combine(tiles - 1)
    send(tiles - 1)

    @pl.loop(0, tiles)
    def _(c):
        total = pair[c, seat].astype(F32)
        for s in range(1, pairs):
            k = lax.rem(seat + s, pairs)
            remote(pair.at[c, k], got.at[c, k], p_send.at[c, 0], p_recv.at[c, k],
                   2 * k + core).wait_recv()
            total = total + got[c, k].astype(F32)
        d_trunk[:, pl.ds(pl.multiple_of(c * tile, tile), tile)] = total.astype(BF16)

    own.wait()
    for s in range(1, n_e):
        j = plane(s)
        remote(d_gate.at[j], gate_back.at[j], g_send.at[0], g_recv.at[j], j).wait_recv()
    for s in range(1, n_e):
        gate_out(s).wait_send()

    @pl.loop(0, tiles)
    def _(c):
        near_out(c).wait_send()
        for s in range(1, pairs):
            part_out(c, s).wait_send()


def return_all(d_pre, first, d_gate):
    n_e = lax.axis_size("expert")
    tile = 512
    depth, width = first.shape
    tiles = depth // tile
    share = d_pre.shape[0] // n_e
    hbm = pl.BlockSpec(memory_space=pltpu.HBM)
    vmem = pl.BlockSpec(memory_space=pltpu.VMEM)
    dma = pltpu.SemaphoreType.DMA
    return pl.pallas_call(
        functools.partial(return_kernel, n_e),
        out_shape=(
            jax.ShapeDtypeStruct((share, depth), BF16),
            jax.ShapeDtypeStruct(d_gate.shape, F32),
        ),
        in_specs=[vmem, hbm, vmem],
        out_specs=(vmem, vmem),
        scratch_shapes=[
            pltpu.VMEM((tiles, tile, width), BF16),
            pltpu.VMEM((tiles, n_e // 2, 2, share, tile), BF16),
            pltpu.VMEM((tiles, n_e // 2, share, tile), BF16),
            pltpu.VMEM((tiles, n_e // 2, share, tile), BF16),
            pltpu.VMEM((tiles, n_e // 2, share, tile), BF16),
            dma((tiles,)), dma((tiles,)), dma((tiles,)),
            dma((tiles, n_e // 2)), dma((tiles, n_e // 2)),
            dma((n_e,)), dma((n_e,)), dma,
        ],
        compiler_params=pltpu.CompilerParams(
            collective_id=1, has_side_effects=True, vmem_limit_bytes=48 * 1024 * 1024),
    )(d_pre, first.reshape(tiles, tile, width), d_gate)


def on_device(trunk, w_first, w_second, gates, d_mixed):
    rank = lax.axis_index("dp")
    first = w_first[0]
    second = w_second[0]
    gate_here = gates[0]
    n_dp = lax.axis_size("dp")
    depth = first.shape[0] // n_dp
    units = second.shape[0] // n_dp
    group = gate_here.shape[1]

    n_e = lax.axis_size("expert")
    gate_parts = gate_here.T.astype(F32).reshape(n_e, -1, gate_here.shape[0])
    rows_all, d_output_all, pre, gates_each, outs_each = gather_all(
        trunk, gate_parts, jnp.transpose(d_mixed, (1, 0, 2)), first, second)
    rows_all = rows_all.reshape(-1, trunk.shape[1])
    d_output_all = d_output_all.reshape(-1, second.shape[1])
    pre = pre.reshape(-1, first.shape[1])
    gates_each = gates_each.astype(BF16)
    d_hidden = lax.dot_general(
        d_output_all, second, (((1,), (1,)), ((), ())), preferred_element_type=F32
    )
    sig = jax.nn.sigmoid(pre)
    d_pre = (d_hidden * sig * (1.0 + pre * (1.0 - sig))).astype(BF16)
    d_pre_here = lax.dynamic_slice_in_dim(d_pre, rank * group, group, 0)
    mixed = jnp.einsum(
        "ert,ero->rto", gates_each, outs_each, preferred_element_type=F32
    ).astype(BF16)
    d_gate_each = jnp.einsum(
        "rto,ero->ert", d_mixed, outs_each, preferred_element_type=F32
    ).astype(BF16)
    d_trunk, back_gate = return_all(d_pre_here, first, d_gate_each.astype(F32))
    d_gate = back_gate.reshape(group, -1).T.astype(BF16)[None]

    columns = lax.dynamic_slice_in_dim(rows_all, rank * depth, depth, 1)
    d_first = lax.dot_general(
        columns, d_pre, (((0,), (0,)), ((), ())), preferred_element_type=F32
    ).astype(BF16)
    some_pre = lax.dynamic_slice_in_dim(pre, rank * units, units, 1)
    some_hidden = jax.nn.silu(some_pre).astype(BF16)
    d_second = lax.dot_general(
        some_hidden, d_output_all, (((0,), (0,)), ((), ())), preferred_element_type=F32
    ).astype(BF16)
    return (mixed, d_trunk, d_gate, d_first[None], d_second[None])


def solution(mesh):
    in_specs = (
        P(("dp", "expert"), None),
        P("expert", None, None),
        P("expert", None, None),
        P("expert", None, "dp"),
        P(("dp", "expert"), None, None),
    )
    out_specs = (
        P(("dp", "expert"), None, None),
        P(("dp", "expert"), None),
        P("expert", None, "dp"),
        P("expert", "dp", None),
        P("expert", "dp", None),
    )
    return jax.shard_map(
        on_device, mesh=mesh, in_specs=in_specs, out_specs=out_specs, check_vma=False
    )
```
